32 devices in a mesh: pts: 2 (over core), cen: 16 (over z, y, x).
Axes of the slice: x: 2, y: 2, z: 4, core: 2. Of those that a mesh axis runs over, the one named last changes fastest.
Arguments:
- points: bfloat16 [2, 1024, 256], P(None, ('pts', 'cen')), may hold values from -4096 to 4096, as said below
- centroids: float32 [16384, 256], P('cen'), may hold values from -6 to 6, as said below
Outputs:
- new_centroids: float32 [16384, 256], P('cen')
- energy: float32 [2, 1024], P(None, 'pts')
The draws below stay inside these ranges and needn't reach their ends.
Inputs may be any that keep to these rules, and one draw needn't show every extreme that they name: Real-valued points. Real-valued centroids.
All inputs are finite; a program needn't handle non-finite values.
Results may differ from the reference program's by a relative error of at most 0.0003.
The reference program's roundings to bfloat16 on the way count: a program that leaves them out, or rounds other values in their place, can miss the bound.
Values may be sent and summed in bfloat16 or wider, within the bound.
A program may use at most 64 MiB of HBM per device.

```python
import jax
import jax.numpy as jnp
from jax import lax

D = 256
PTS_DEV = 32
STEPS = 2
K = 16384
BATCH = 1024
N_CEN = 16


def centroid_table(key):
    return jax.random.normal(jax.random.fold_in(key, 11), (K, D), jnp.float32)


def draw_centroids(key, part):
    return jnp.clip(centroid_table(key), -6.0, 6.0)


def draw_points(key, part):
    base = jax.random.normal(jax.random.fold_in(key, 23), (STEPS, BATCH, D), jnp.float32)
    table = jnp.clip(centroid_table(key), -6.0, 6.0)
    picks = jax.random.randint(jax.random.fold_in(key, 31), (STEPS, BATCH), 0, K)
    order = jnp.arange(BATCH)
    target = (150.0 + 100.0 * (order % 3)).astype(jnp.float32)
    noise = 0.1
    chosen = order % 61 == 0
    picked = table[picks]
    norm_sq = jnp.sum(picked * picked, axis=2)
    strength = 0.5 * (32.0 * target[None, :] / norm_sq + 1.0)
    aligned = picked * strength[:, :, None] + noise * base
    base = jnp.where(chosen[None, :, None], aligned, base)
    return jnp.clip(base, -4096.0, 4096.0).astype(jnp.bfloat16)


def setup_inputs(seed: int = 0) -> dict:
    keys = jax.random.split(jax.random.key(seed), 3)
    points = draw_points(jax.random.fold_in(keys[2], 71), 0)
    centroids = draw_centroids(jax.random.fold_in(keys[2], 71), 0)
    return dict(points=points, centroids=centroids)


TEMPER = 32.0


def reference(points, centroids):
    current = centroids
    energies = []
    for iteration in range(STEPS):
        cent_low = current.astype(jnp.bfloat16)
        cent_sq = jnp.sum(current * current, axis=1)
        blocks = points[iteration].reshape(BATCH // (PTS_DEV * N_CEN), PTS_DEV * N_CEN, D)

        def one_block(carry, rows_blk):
            sums, counts = carry
            inner = lax.dot_general(rows_blk, cent_low, (((1,), (1,)), ((), ())), preferred_element_type=jnp.float32)
            logits = (2.0 * inner - cent_sq[None, :]) / TEMPER
            top = jnp.max(logits, axis=1)
            weights = jnp.exp(logits - top[:, None])
            total = jnp.sum(weights, axis=1)
            resp = weights / total[:, None]
            counts = counts + jnp.sum(resp, axis=0)
            sums = sums + lax.dot_general(resp.astype(jnp.bfloat16), rows_blk, (((0,), (0,)), ((), ())), preferred_element_type=jnp.float32)
            return (sums, counts), top + jnp.log(total)

        start_carry = (jnp.zeros((K, D), jnp.float32), jnp.zeros((K,), jnp.float32))
        (sums, counts), block_energy = lax.scan(one_block, start_carry, blocks)
        current = (current + sums) / (1.0 + counts)[:, None]
        energies.append(block_energy.reshape(BATCH))
    return current, jnp.stack(energies)
```

```python
import functools

import jax
import jax.numpy as jnp
from jax import lax
from jax.experimental import pallas as pl
from jax.experimental.pallas import tpu as pltpu
from jax.sharding import PartitionSpec as P

TEMPER = 32.0
MESH = pl.DeviceIdType.MESH
LANES = 128
ROWS = 256


def split(n):
    near = 1
    while near * near * 4 <= n:
        near *= 2
    if n % near:
        near = 1
    return n // near, near


def kernel(far, near, n_pts, pts_ref, cen_ref, out_ref, en_ref,
           x_ref, w_ref, cur_ref, low_ref, sq_ref, stat1, stat2, got,
           z_send, q_send, p_recv, s1_send, s1_recv, s2_send, s2_recv, c_send, c_recv):
    steps, own, dim = pts_ref.shape
    k_loc = cen_ref.shape[0]
    n_blk = k_loc // ROWS
    width = near * own
    cols = width // LANES
    groups = far * cols
    cen = lax.axis_index("cen")
    p = lax.axis_index("pts")
    a = cen // near
    b = lax.rem(cen, near)
    far_peers = [lax.rem(a + d, far) for d in range(1, far)]
    near_peers = [lax.rem(b + d, near) for d in range(1, near)]
    pts_peers = [lax.rem(p + d, n_pts) for d in range(1, n_pts)]

    barrier = pltpu.get_barrier_semaphore()
    for peer in far_peers:
        pl.semaphore_signal(barrier, inc=1, device_id={"cen": peer * near + b}, device_id_type=MESH)
    for peer in near_peers:
        pl.semaphore_signal(barrier, inc=1, device_id={"cen": a * near + peer}, device_id_type=MESH)
    for peer in pts_peers:
        pl.semaphore_signal(barrier, inc=1, device_id={"pts": peer}, device_id_type=MESH)

    def prepare(rows, value):
        cur_ref[rows, :] = value
        low = value.astype(jnp.bfloat16).astype(jnp.float32) * (2.0 / TEMPER)
        low_ref[rows, :] = low.astype(jnp.bfloat16)
        sq = jnp.sum(value * value, axis=1, keepdims=True) * (1.0 / TEMPER)
        sq_ref[rows, :] = jnp.broadcast_to(sq, (ROWS, LANES))

    for s in range(steps):
        x_ref[s, a, pl.ds(b * own, own), :] = pts_ref[s]

    @pl.loop(0, n_blk)
    def _(blk):
        rows = pl.ds(pl.multiple_of(blk * ROWS, ROWS), ROWS)
        prepare(rows, cen_ref[rows, :])

    pl.semaphore_wait(barrier, len(far_peers) + len(near_peers) + len(pts_peers))

    def chunk(s, i, j):
        return x_ref.at[s, i, pl.ds(j * own, own), :]

    def far_copy(s, d):
        peer = lax.rem(a + d, far)
        return pltpu.make_async_remote_copy(
            src_ref=pts_ref.at[s], dst_ref=chunk(s, a, b),
            send_sem=z_send.at[s, d], recv_sem=p_recv.at[s, a, b],
            device_id={"cen": peer * near + b}, device_id_type=MESH)

    def near_copy(s, i, d):
        peer = lax.rem(b + d, near)
        return pltpu.make_async_remote_copy(
            src_ref=chunk(s, i, b), dst_ref=chunk(s, i, b),
            send_sem=q_send.at[s, i, d], recv_sem=p_recv.at[s, i, b],
            device_id={"cen": a * near + peer}, device_id_type=MESH)

    def own_near_copy(s, d):
        peer = lax.rem(b + d, near)
        return pltpu.make_async_remote_copy(
            src_ref=pts_ref.at[s], dst_ref=chunk(s, a, b),
            send_sem=q_send.at[s, a, d], recv_sem=p_recv.at[s, a, b],
            device_id={"cen": a * near + peer}, device_id_type=MESH)

    def arrived(s, i, j):
        pltpu.make_async_remote_copy(
            src_ref=chunk(s, i, j), dst_ref=chunk(s, i, j),
            send_sem=z_send.at[s, 0], recv_sem=p_recv.at[s, i, j],
            device_id={"cen": cen}, device_id_type=MESH).wait_recv()

    def send_own(s):
        for d in range(1, far):
            far_copy(s, d).start()
        for d in range(1, near):
            own_near_copy(s, d).start()

    def forward(s):
        for d in range(1, far):
            i = lax.rem(a - d + far, far)
            arrived(s, i, b)
            for e in range(1, near):
                near_copy(s, i, e).start()

    def stat1_copy(s, d):
        peer = lax.rem(a + d, far)
        return pltpu.make_async_remote_copy(
            src_ref=stat1.at[s, a], dst_ref=stat1.at[s, a],
            send_sem=s1_send.at[s, d], recv_sem=s1_recv.at[s, a],
            device_id={"cen": peer * near + b}, device_id_type=MESH)

    def stat2_copy(s, d):
        peer = lax.rem(b + d, near)
        return pltpu.make_async_remote_copy(
            src_ref=stat2.at[s, b], dst_ref=stat2.at[s, b],
            send_sem=s2_send.at[s, d], recv_sem=s2_recv.at[s, b],
            device_id={"cen": a * near + peer}, device_id_type=MESH)

    def sums_copy(s, d, blk):
        peer = lax.rem(p + d, n_pts)
        return pltpu.make_async_remote_copy(
            src_ref=got.at[s, p, blk], dst_ref=got.at[s, p, blk],
            send_sem=c_send.at[s, d, blk], recv_sem=c_recv.at[s, p, blk],
            device_id={"pts": peer}, device_id_type=MESH)

    def landed(ref, sem):
        pltpu.make_async_remote_copy(
            src_ref=ref, dst_ref=ref, send_sem=z_send.at[0, 0], recv_sem=sem,
            device_id={"cen": cen}, device_id_type=MESH).wait_recv()

    def joined(stat, s, n):
        top = stat[s, 0, 0]
        for i in range(1, n):
            top = jnp.maximum(top, stat[s, i, 0])
        total = stat[s, 0, 1] * jnp.exp(stat[s, 0, 0] - top)
        for i in range(1, n):
            total = total + stat[s, i, 1] * jnp.exp(stat[s, i, 0] - top)
        return top, total

    send_own(0)
    forward(0)
    send_own(1) if steps > 1 else None

    for s in range(steps):
        def one_group(d, carry):
            i = lax.rem(a + d, far)
            for e in range(1, near):
                arrived(s, i, lax.rem(b + e, near))
            for j in range(cols):
                xg = x_ref[s, i, j * LANES:(j + 1) * LANES, :]
                logits = lax.dot_general(
                    low_ref[...], xg, (((1,), (1,)), ((), ())),
                    preferred_element_type=jnp.float32) - sq_ref[...]
                top = jnp.max(logits, axis=0, keepdims=True)
                weights = jnp.exp(logits - top)
                g = i * cols + j
                w_ref[:, pl.ds(pl.multiple_of(g * LANES, LANES), LANES)] = weights
                stat1[s, a, 0, pl.ds(g, 1), :] = top
                stat1[s, a, 1, pl.ds(g, 1), :] = jnp.sum(weights, axis=0, keepdims=True)
            return carry

        lax.fori_loop(0, far, one_group, 0)
        for d in range(1, far):
            stat1_copy(s, d).start()
        if s + 1 < steps:
            forward(s + 1)
            if s + 2 < steps:
                send_own(s + 2)
        for d in range(1, far):
            i = lax.rem(a - d + far, far)
            landed(stat1.at[s, i], s1_recv.at[s, i])
        top, total = joined(stat1, s, far)
        stat2[s, b, 0] = top
        stat2[s, b, 1] = total
        for d in range(1, near):
            stat2_copy(s, d).start()
        for d in range(1, near):
            i = lax.rem(b - d + near, near)
            landed(stat2.at[s, i], s2_recv.at[s, i])
        top, total = joined(stat2, s, near)
        energy = top + jnp.log(total)
        scale = jnp.exp(stat1[s, a, 0] - top) / total
        for g in range(groups):
            en_ref[s:s + 1, g * LANES:(g + 1) * LANES] = energy[g:g + 1, :]
        scale = jnp.concatenate([scale[g:g + 1, :] for g in range(groups)], axis=1)

        @pl.loop(0, n_blk)
        def _(blk):
            rows = pl.ds(pl.multiple_of(blk * ROWS, ROWS), ROWS)
            resp = w_ref[rows, :] * scale
            part = resp[:, :LANES]
            for g in range(1, groups):
                part = part + resp[:, g * LANES:(g + 1) * LANES]
            count = jnp.sum(jnp.transpose(part), axis=0, keepdims=True)
            xs = x_ref[s].reshape(far * width, dim)
            sums = lax.dot_general(
                resp.astype(jnp.bfloat16), xs, (((1,), (0,)), ((), ())),
                preferred_element_type=jnp.float32)
            got[s, p, blk, :ROWS, :] = sums
            got[s, p, blk, ROWS:ROWS + 1, :] = count
            for d in range(1, n_pts):
                sums_copy(s, d, blk).start()

        @pl.loop(0, n_blk)
        def _(blk):
            rows = pl.ds(pl.multiple_of(blk * ROWS, ROWS), ROWS)
            for d in range(1, n_pts):
                i = lax.rem(p + d, n_pts)
                landed(got.at[s, i, blk], c_recv.at[s, i, blk])
            sums = got[s, 0, blk, :ROWS, :]
            count = got[s, 0, blk, ROWS:ROWS + 1, :]
            for i in range(1, n_pts):
                sums = sums + got[s, i, blk, :ROWS, :]
                count = count + got[s, i, blk, ROWS:ROWS + 1, :]
            column = jnp.transpose(jnp.broadcast_to(1.0 + count, (LANES, ROWS)))
            column = jnp.concatenate([column] * (dim // LANES), axis=1)
            value = (cur_ref[rows, :] + sums) / column
            if s + 1 < steps:
                prepare(rows, value)
            else:
                out_ref[rows, :] = value

    for s in range(steps):
        for d in range(1, far):
            far_copy(s, d).wait_send()
            stat1_copy(s, d).wait_send()
            for e in range(1, near):
                near_copy(s, lax.rem(a + d, far), e).wait_send()
        for d in range(1, near):
            own_near_copy(s, d).wait_send()
            stat2_copy(s, d).wait_send()

        @pl.loop(0, n_blk)
        def _(blk):
            for d in range(1, n_pts):
                sums_copy(s, d, blk).wait_send()


def on_device(far, near, n_pts, points, centroids):
    steps, own, dim = points.shape
    k_loc = centroids.shape[0]
    n_blk = k_loc // ROWS
    batch = far * near * own
    groups = batch // LANES
    vmem = pl.BlockSpec(memory_space=pltpu.VMEM)
    dma = pltpu.SemaphoreType.DMA
    return pl.pallas_call(
        functools.partial(kernel, far, near, n_pts),
        out_shape=(jax.ShapeDtypeStruct((k_loc, dim), jnp.float32),
                   jax.ShapeDtypeStruct((steps, batch), jnp.float32)),
        in_specs=[vmem, vmem],
        out_specs=(vmem, vmem),
        scratch_shapes=[
            pltpu.VMEM((steps, far, near * own, dim), jnp.bfloat16),
            pltpu.VMEM((k_loc, batch), jnp.float32),
            pltpu.VMEM((k_loc, dim), jnp.float32),
            pltpu.VMEM((k_loc, dim), jnp.bfloat16),
            pltpu.VMEM((k_loc, LANES), jnp.float32),
            pltpu.VMEM((steps, far, 2, groups, LANES), jnp.float32),
            pltpu.VMEM((steps, near, 2, groups, LANES), jnp.float32),
            pltpu.VMEM((steps, n_pts, n_blk, ROWS + 8, dim), jnp.float32),
            dma((steps, far)),
            dma((steps, far, near)),
            dma((steps, far, near)),
            dma((steps, far)),
            dma((steps, far)),
            dma((steps, near)),
            dma((steps, near)),
            dma((steps, n_pts, n_blk)),
            dma((steps, n_pts, n_blk)),
        ],
        compiler_params=pltpu.CompilerParams(
            collective_id=0, has_side_effects=True, vmem_limit_bytes=60 * 1024 * 1024),
    )(points, centroids)


def solution(mesh):
    far, near = split(mesh.shape["cen"])
    placed = (P(None, ("pts", "cen"), None), P("cen", None))
    return jax.shard_map(
        functools.partial(on_device, far, near, mesh.shape["pts"]),
        mesh=mesh,
        in_specs=placed,
        out_specs=(P("cen", None), P(None, "pts")),
        check_vma=False,
    )
```

```python
import functools

import jax
import jax.numpy as jnp
from jax import lax
from jax.experimental import pallas as pl
from jax.experimental.pallas import tpu as pltpu
from jax.sharding import PartitionSpec as P

TEMPER = 32.0
MESH = pl.DeviceIdType.MESH
LANES = 128
ROWS = 256


def split(n):
    near = 1
    while near * near * 4 <= n:
        near *= 2
    assert n % near == 0 and (n // near) & (n // near - 1) == 0
    return n // near, near


def flip(i, d):
    bit = 1
    while bit <= d:
        if d & bit:
            i = i + bit - 2 * bit * lax.rem(i // bit, 2)
        bit *= 2
    return i


def kernel(far, near, n_pts, pts_ref, cen_ref, out_ref, en_ref,
           x_ref, w_ref, cur_ref, low_ref, sq_ref, stat1, stat2, got,
           z_send, q_send, p_recv, s1_send, s1_recv, s2_send, s2_recv, c_send, c_recv,
           in_sem, cen_sem):
    steps, own, dim = pts_ref.shape
    k_loc = cen_ref.shape[0]
    n_blk = k_loc // ROWS
    width = near * own
    cols = width // LANES
    groups = far * cols
    cen = lax.axis_index("cen")
    p = lax.axis_index("pts")
    a = cen // near
    b = lax.rem(cen, near)
    far_peers = [flip(a, d) for d in range(1, far)]
    near_peers = [flip(b, d) for d in range(1, near)]
    pts_peers = [lax.rem(p + d, n_pts) for d in range(1, n_pts)]

    barrier = pltpu.get_barrier_semaphore()
    for peer in far_peers:
        pl.semaphore_signal(barrier, inc=1, device_id={"cen": peer * near + b}, device_id_type=MESH)
    for peer in near_peers:
        pl.semaphore_signal(barrier, inc=1, device_id={"cen": a * near + peer}, device_id_type=MESH)
    for peer in pts_peers:
        pl.semaphore_signal(barrier, inc=1, device_id={"pts": peer}, device_id_type=MESH)

    def prepare(rows, value):
        low = value.astype(jnp.bfloat16).astype(jnp.float32) * (2.0 / TEMPER)
        low_ref[rows, :] = low.astype(jnp.bfloat16)
        sq = jnp.sum(value * value, axis=1, keepdims=True) * (1.0 / TEMPER)
        sq_ref[rows, :] = jnp.broadcast_to(sq, (ROWS, LANES))

    def cen_copy(blk):
        rows = pl.ds(pl.multiple_of(blk * ROWS, ROWS), ROWS)
        return pltpu.make_async_copy(cen_ref.at[rows, :], cur_ref.at[rows, :], cen_sem.at[blk])

    def pts_copy(s):
        return pltpu.make_async_copy(pts_ref.at[s], x_ref.at[s, a, pl.ds(b * own, own), :], in_sem.at[s])

    for s in range(steps):
        pts_copy(s).start()

    @pl.loop(0, n_blk)
    def _(blk):
        cen_copy(blk).start()

    for s in range(steps):
        pts_copy(s).wait()

    @pl.loop(0, n_blk)
    def _(blk):
        cen_copy(blk).wait()
        rows = pl.ds(pl.multiple_of(blk * ROWS, ROWS), ROWS)
        prepare(rows, cur_ref[rows, :])

    pl.semaphore_wait(barrier, len(far_peers) + len(near_peers) + len(pts_peers))

    def chunk(s, i, j):
        return x_ref.at[s, i, pl.ds(j * own, own), :]

    def far_copy(s, d):
        peer = flip(a, d)
        return pltpu.make_async_remote_copy(
            src_ref=chunk(s, a, b), dst_ref=chunk(s, a, b),
            send_sem=z_send.at[s, d], recv_sem=p_recv.at[s, a, b],
            device_id={"cen": peer * near + b}, device_id_type=MESH)

    def near_copy(s, i, d):
        peer = flip(b, d)
        return pltpu.make_async_remote_copy(
            src_ref=chunk(s, i, b), dst_ref=chunk(s, i, b),
            send_sem=q_send.at[s, i, d], recv_sem=p_recv.at[s, i, b],
            device_id={"cen": a * near + peer}, device_id_type=MESH)

    def own_near_copy(s, d):
        peer = flip(b, d)
        return pltpu.make_async_remote_copy(
            src_ref=chunk(s, a, b), dst_ref=chunk(s, a, b),
            send_sem=q_send.at[s, a, d], recv_sem=p_recv.at[s, a, b],
            device_id={"cen": a * near + peer}, device_id_type=MESH)

    def arrived(s, i, j):
        pltpu.make_async_remote_copy(
            src_ref=chunk(s, i, j), dst_ref=chunk(s, i, j),
            send_sem=z_send.at[s, 0], recv_sem=p_recv.at[s, i, j],
            device_id={"cen": cen}, device_id_type=MESH).wait_recv()

    def send_own(s):
        for d in reversed(range(1, far)):
            far_copy(s, d).start()
        for d in reversed(range(1, near)):
            own_near_copy(s, d).start()

    def forward(s):
        for d in range(1, far):
            i = flip(a, d)
            arrived(s, i, b)
            for e in reversed(range(1, near)):
                near_copy(s, i, e).start()

    def stat1_copy(s, d):
        peer = flip(a, d)
        return pltpu.make_async_remote_copy(
            src_ref=stat1.at[s, a], dst_ref=stat1.at[s, a],
            send_sem=s1_send.at[s, d], recv_sem=s1_recv.at[s, a],
            device_id={"cen": peer * near + b}, device_id_type=MESH)

    def stat2_copy(s, d):
        peer = flip(b, d)
        return pltpu.make_async_remote_copy(
            src_ref=stat2.at[s, b], dst_ref=stat2.at[s, b],
            send_sem=s2_send.at[s, d], recv_sem=s2_recv.at[s, b],
            device_id={"cen": a * near + peer}, device_id_type=MESH)

    def sums_copy(s, d, blk):
        peer = lax.rem(p + d, n_pts)
        return pltpu.make_async_remote_copy(
            src_ref=got.at[s, p, blk], dst_ref=got.at[s, p, blk],
            send_sem=c_send.at[s, d, blk], recv_sem=c_recv.at[s, p, blk],
            device_id={"pts": peer}, device_id_type=MESH)

    def landed(ref, sem):
        pltpu.make_async_remote_copy(
            src_ref=ref, dst_ref=ref, send_sem=z_send.at[0, 0], recv_sem=sem,
            device_id={"cen": cen}, device_id_type=MESH).wait_recv()

    def joined(stat, s, n):
        top = stat[s, 0, 0]
        for i in range(1, n):
            top = jnp.maximum(top, stat[s, i, 0])
        total = stat[s, 0, 1] * jnp.exp(stat[s, 0, 0] - top)
        for i in range(1, n):
            total = total + stat[s, i, 1] * jnp.exp(stat[s, i, 0] - top)
        return top, total

    send_own(0)
    forward(0)
    send_own(1) if steps > 1 else None

    for s in range(steps):
        def one_group(i):
            for e in range(1, near):
                arrived(s, i, flip(b, e))
            for j in range(cols):
                xg = x_ref[s, i, j * LANES:(j + 1) * LANES, :]
                logits = lax.dot_general(
                    low_ref[...], xg, (((1,), (1,)), ((), ())),
                    preferred_element_type=jnp.float32) - sq_ref[...]
                top = jnp.max(logits, axis=0, keepdims=True)
                weights = jnp.exp(logits - top)
                g = i * cols + j
                w_ref[:, pl.ds(pl.multiple_of(g * LANES, LANES), LANES)] = weights
                stat1[s, a, 0, pl.ds(g, 1), :] = top
                stat1[s, a, 1, pl.ds(g, 1), :] = jnp.sum(weights, axis=0, keepdims=True)

        for d in range(far):
            one_group(flip(a, d))
        for d in reversed(range(1, far)):
            stat1_copy(s, d).start()
        if s + 1 < steps:
            forward(s + 1)
            if s + 2 < steps:
                send_own(s + 2)
        for d in range(1, far):
            i = flip(a, d)
            landed(stat1.at[s, i], s1_recv.at[s, i])
        top, total = joined(stat1, s, far)
        stat2[s, b, 0] = top
        stat2[s, b, 1] = total
        for d in reversed(range(1, near)):
            stat2_copy(s, d).start()
        for d in range(1, near):
            i = flip(b, d)
            landed(stat2.at[s, i], s2_recv.at[s, i])
        top, total = joined(stat2, s, near)
        energy = top + jnp.log(total)
        scale = jnp.exp(stat1[s, a, 0] - top) / total
        for g in range(groups):
            en_ref[s:s + 1, g * LANES:(g + 1) * LANES] = energy[g:g + 1, :]
        scale = jnp.concatenate([scale[g:g + 1, :] for g in range(groups)], axis=1)

        @pl.loop(0, n_blk)
        def _(blk):
            rows = pl.ds(pl.multiple_of(blk * ROWS, ROWS), ROWS)
            resp = w_ref[rows, :] * scale
            part = resp[:, :LANES]
            for g in range(1, groups):
                part = part + resp[:, g * LANES:(g + 1) * LANES]
            count = jnp.sum(jnp.transpose(part), axis=0, keepdims=True)
            xs = x_ref[s].reshape(far * width, dim)
            sums = lax.dot_general(
                resp.astype(jnp.bfloat16), xs, (((1,), (0,)), ((), ())),
                preferred_element_type=jnp.float32)
            got[s, p, blk, :ROWS, :] = sums
            got[s, p, blk, ROWS:ROWS + 1, :] = count
            for d in range(1, n_pts):
                sums_copy(s, d, blk).start()

        @pl.loop(0, n_blk)
        def _(blk):
            rows = pl.ds(pl.multiple_of(blk * ROWS, ROWS), ROWS)
            for d in range(1, n_pts):
                i = lax.rem(p + d, n_pts)
                landed(got.at[s, i, blk], c_recv.at[s, i, blk])
            sums = got[s, 0, blk, :ROWS, :]
            count = got[s, 0, blk, ROWS:ROWS + 1, :]
            for i in range(1, n_pts):
                sums = sums + got[s, i, blk, :ROWS, :]
                count = count + got[s, i, blk, ROWS:ROWS + 1, :]
            column = jnp.transpose(jnp.broadcast_to(1.0 + count, (LANES, ROWS)))
            column = jnp.concatenate([column] * (dim // LANES), axis=1)
            value = (cur_ref[rows, :] + sums) / column
            if s + 1 < steps:
                cur_ref[rows, :] = value
                prepare(rows, value)
            else:
                out_ref[rows, :] = value

    for s in range(steps):
        for d in range(1, far):
            far_copy(s, d).wait_send()
            stat1_copy(s, d).wait_send()
            for e in range(1, near):
                near_copy(s, flip(a, d), e).wait_send()
        for d in range(1, near):
            own_near_copy(s, d).wait_send()
            stat2_copy(s, d).wait_send()

        @pl.loop(0, n_blk)
        def _(blk):
            for d in range(1, n_pts):
                sums_copy(s, d, blk).wait_send()


def on_device(far, near, n_pts, points, centroids):
    steps, own, dim = points.shape
    k_loc = centroids.shape[0]
    n_blk = k_loc // ROWS
    batch = far * near * own
    groups = batch // LANES
    vmem = pl.BlockSpec(memory_space=pltpu.VMEM)
    dma = pltpu.SemaphoreType.DMA
    return pl.pallas_call(
        functools.partial(kernel, far, near, n_pts),
        out_shape=(pltpu.VMEM((k_loc, dim), jnp.float32),
                   pltpu.VMEM((steps, batch), jnp.float32)),
        in_specs=[pl.BlockSpec(memory_space=pl.ANY)] * 2,
        out_specs=(vmem, vmem),
        scratch_shapes=[
            pltpu.VMEM((steps, far, near * own, dim), jnp.bfloat16),
            pltpu.VMEM((k_loc, batch), jnp.float32),
            pltpu.VMEM((k_loc, dim), jnp.float32),
            pltpu.VMEM((k_loc, dim), jnp.bfloat16),
            pltpu.VMEM((k_loc, LANES), jnp.float32),
            pltpu.VMEM((steps, far, 2, groups, LANES), jnp.float32),
            pltpu.VMEM((steps, near, 2, groups, LANES), jnp.float32),
            pltpu.VMEM((steps, n_pts, n_blk, ROWS + 8, dim), jnp.float32),
            dma((steps, far)),
            dma((steps, far, near)),
            dma((steps, far, near)),
            dma((steps, far)),
            dma((steps, far)),
            dma((steps, near)),
            dma((steps, near)),
            dma((steps, n_pts, n_blk)),
            dma((steps, n_pts, n_blk)),
            dma((steps,)),
            dma((n_blk,)),
        ],
        compiler_params=pltpu.CompilerParams(
            collective_id=0, has_side_effects=True, vmem_limit_bytes=60 * 1024 * 1024),
    )(points, centroids)


def solution(mesh):
    far, near = split(mesh.shape["cen"])
    placed = (P(None, ("pts", "cen"), None), P("cen", None))
    return jax.shard_map(
        functools.partial(on_device, far, near, mesh.shape["pts"]),
        mesh=mesh,
        in_specs=placed,
        out_specs=(P("cen", None), P(None, "pts")),
        check_vma=False,
    )
```

```python
import functools

import jax
import jax.numpy as jnp
from jax import lax
from jax.experimental import pallas as pl
from jax.experimental.pallas import tpu as pltpu
from jax.sharding import PartitionSpec as P

TEMPER = 32.0
MESH = pl.DeviceIdType.MESH
LANES = 128
ROWS = 256


def split(n):
    near = 1
    while near * near * 4 <= n:
        near *= 2
    assert n % near == 0 and (n // near) & (n // near - 1) == 0
    return n // near, near


def flip(i, d):
    bit = 1
    while bit <= d:
        if d & bit:
            i = i + bit - 2 * bit * lax.rem(i // bit, 2)
        bit *= 2
    return i


def kernel(far, near, n_pts, pts_ref, cen_ref, out_ref, en_ref,
           x_ref, w_ref, cur_ref, low_ref, sq_ref, stat, got,
           z_send, q_send, p_recv, s_send, s_recv, c_send, c_recv,
           in_sem, cen_sem):
    steps, own, dim = pts_ref.shape
    k_loc = cen_ref.shape[0]
    n_blk = k_loc // ROWS
    width = near * own
    cols = width // LANES
    groups = far * cols
    cen = lax.axis_index("cen")
    p = lax.axis_index("pts")
    a = cen // near
    b = lax.rem(cen, near)
    far_peers = [flip(a, d) for d in range(1, far)]
    near_peers = [flip(b, d) for d in range(1, near)]
    pts_peers = [lax.rem(p + d, n_pts) for d in range(1, n_pts)]

    barrier = pltpu.get_barrier_semaphore()
    for peer in far_peers:
        pl.semaphore_signal(barrier, inc=1, device_id={"cen": peer * near + b}, device_id_type=MESH)
    for peer in near_peers:
        pl.semaphore_signal(barrier, inc=1, device_id={"cen": a * near + peer}, device_id_type=MESH)
    for peer in pts_peers:
        pl.semaphore_signal(barrier, inc=1, device_id={"pts": peer}, device_id_type=MESH)

    def prepare(rows, value):
        low = value.astype(jnp.bfloat16).astype(jnp.float32) * (2.0 / TEMPER)
        low_ref[rows, :] = low.astype(jnp.bfloat16)
        sq = jnp.sum(value * value, axis=1, keepdims=True) * (1.0 / TEMPER)
        sq_ref[rows, :] = jnp.broadcast_to(sq, (ROWS, LANES))

    def cen_copy(blk):
        rows = pl.ds(pl.multiple_of(blk * ROWS, ROWS), ROWS)
        return pltpu.make_async_copy(cen_ref.at[rows, :], cur_ref.at[rows, :], cen_sem.at[blk])

    def pts_copy(s):
        return pltpu.make_async_copy(pts_ref.at[s], x_ref.at[s, a, pl.ds(b * own, own), :], in_sem.at[s])

    for s in range(steps):
        pts_copy(s).start()

    @pl.loop(0, n_blk)
    def _(blk):
        cen_copy(blk).start()

    for s in range(steps):
        pts_copy(s).wait()

    @pl.loop(0, n_blk)
    def _(blk):
        cen_copy(blk).wait()
        rows = pl.ds(pl.multiple_of(blk * ROWS, ROWS), ROWS)
        prepare(rows, cur_ref[rows, :])

    pl.semaphore_wait(barrier, len(far_peers) + len(near_peers) + len(pts_peers))

    def chunk(s, i, j):
        return x_ref.at[s, i, pl.ds(j * own, own), :]

    def far_copy(s, d):
        peer = flip(a, d)
        return pltpu.make_async_remote_copy(
            src_ref=chunk(s, a, b), dst_ref=chunk(s, a, b),
            send_sem=z_send.at[s, d], recv_sem=p_recv.at[s, a, b],
            device_id={"cen": peer * near + b}, device_id_type=MESH)

    def near_copy(s, i, d):
        peer = flip(b, d)
        return pltpu.make_async_remote_copy(
            src_ref=chunk(s, i, b), dst_ref=chunk(s, i, b),
            send_sem=q_send.at[s, i, d], recv_sem=p_recv.at[s, i, b],
            device_id={"cen": a * near + peer}, device_id_type=MESH)

    def own_near_copy(s, d):
        peer = flip(b, d)
        return pltpu.make_async_remote_copy(
            src_ref=chunk(s, a, b), dst_ref=chunk(s, a, b),
            send_sem=q_send.at[s, a, d], recv_sem=p_recv.at[s, a, b],
            device_id={"cen": a * near + peer}, device_id_type=MESH)

    def arrived(s, i, j):
        pltpu.make_async_remote_copy(
            src_ref=chunk(s, i, j), dst_ref=chunk(s, i, j),
            send_sem=z_send.at[s, 0], recv_sem=p_recv.at[s, i, j],
            device_id={"cen": cen}, device_id_type=MESH).wait_recv()

    def send_own(s):
        for d in reversed(range(1, far)):
            far_copy(s, d).start()
        for d in reversed(range(1, near)):
            own_near_copy(s, d).start()

    def forward(s):
        for d in range(1, far):
            i = flip(a, d)
            arrived(s, i, b)
            for e in reversed(range(1, near)):
                near_copy(s, i, e).start()

    def stat_copy(s, d):
        return pltpu.make_async_remote_copy(
            src_ref=stat.at[s, cen], dst_ref=stat.at[s, cen],
            send_sem=s_send.at[s, d], recv_sem=s_recv.at[s, cen],
            device_id={"cen": flip(cen, d)}, device_id_type=MESH)

    def sums_copy(s, d, blk):
        peer = lax.rem(p + d, n_pts)
        return pltpu.make_async_remote_copy(
            src_ref=got.at[s, p, blk], dst_ref=got.at[s, p, blk],
            send_sem=c_send.at[s, d, blk], recv_sem=c_recv.at[s, p, blk],
            device_id={"pts": peer}, device_id_type=MESH)

    def landed(ref, sem):
        pltpu.make_async_remote_copy(
            src_ref=ref, dst_ref=ref, send_sem=z_send.at[0, 0], recv_sem=sem,
            device_id={"cen": cen}, device_id_type=MESH).wait_recv()

    def joined(s):
        tops = stat[s, :, 0]
        top = jnp.max(tops, axis=0)
        return top, jnp.sum(stat[s, :, 1] * jnp.exp(tops - top[None]), axis=0)

    send_own(0)
    forward(0)
    send_own(1) if steps > 1 else None

    for s in range(steps):
        def one_group(i):
            for e in range(1, near):
                arrived(s, i, flip(b, e))
            for j in range(cols):
                xg = x_ref[s, i, j * LANES:(j + 1) * LANES, :]
                logits = lax.dot_general(
                    low_ref[...], xg, (((1,), (1,)), ((), ())),
                    preferred_element_type=jnp.float32) - sq_ref[...]
                top = jnp.max(logits, axis=0, keepdims=True)
                weights = jnp.exp(logits - top)
                g = i * cols + j
                w_ref[:, pl.ds(pl.multiple_of(g * LANES, LANES), LANES)] = weights
                stat[s, cen, 0, pl.ds(g, 1), :] = top
                stat[s, cen, 1, pl.ds(g, 1), :] = jnp.sum(weights, axis=0, keepdims=True)

        for d in range(far):
            one_group(flip(a, d))
        for d in reversed(range(1, far * near)):
            stat_copy(s, d).start()
        if s + 1 < steps:
            forward(s + 1)
            if s + 2 < steps:
                send_own(s + 2)
        for d in range(1, far * near):
            i = flip(cen, d)
            landed(stat.at[s, i], s_recv.at[s, i])
        top, total = joined(s)
        energy = top + jnp.log(total)
        scale = jnp.exp(stat[s, cen, 0] - top) / total
        for g in range(groups):
            en_ref[s:s + 1, g * LANES:(g + 1) * LANES] = energy[g:g + 1, :]
        scale = jnp.concatenate([scale[g:g + 1, :] for g in range(groups)], axis=1)

        @pl.loop(0, n_blk)
        def _(blk):
            rows = pl.ds(pl.multiple_of(blk * ROWS, ROWS), ROWS)
            resp = w_ref[rows, :] * scale
            part = resp[:, :LANES]
            for g in range(1, groups):
                part = part + resp[:, g * LANES:(g + 1) * LANES]
            count = jnp.sum(jnp.transpose(part), axis=0, keepdims=True)
            xs = x_ref[s].reshape(far * width, dim)
            sums = lax.dot_general(
                resp.astype(jnp.bfloat16), xs, (((1,), (0,)), ((), ())),
                preferred_element_type=jnp.float32)
            got[s, p, blk, :ROWS, :] = sums
            got[s, p, blk, ROWS:ROWS + 1, :] = count
            for d in range(1, n_pts):
                sums_copy(s, d, blk).start()

        @pl.loop(0, n_blk)
        def _(blk):
            rows = pl.ds(pl.multiple_of(blk * ROWS, ROWS), ROWS)
            for d in range(1, n_pts):
                i = lax.rem(p + d, n_pts)
                landed(got.at[s, i, blk], c_recv.at[s, i, blk])
            sums = got[s, 0, blk, :ROWS, :]
            count = got[s, 0, blk, ROWS:ROWS + 1, :]
            for i in range(1, n_pts):
                sums = sums + got[s, i, blk, :ROWS, :]
                count = count + got[s, i, blk, ROWS:ROWS + 1, :]
            column = jnp.transpose(jnp.broadcast_to(1.0 + count, (LANES, ROWS)))
            column = jnp.concatenate([column] * (dim // LANES), axis=1)
            value = (cur_ref[rows, :] + sums) / column
            if s + 1 < steps:
                cur_ref[rows, :] = value
                prepare(rows, value)
            else:
                out_ref[rows, :] = value

    for s in range(steps):
        for d in range(1, far * near):
            stat_copy(s, d).wait_send()
        for d in range(1, far):
            far_copy(s, d).wait_send()
            for e in range(1, near):
                near_copy(s, flip(a, d), e).wait_send()
        for d in range(1, near):
            own_near_copy(s, d).wait_send()

        @pl.loop(0, n_blk)
        def _(blk):
            for d in range(1, n_pts):
                sums_copy(s, d, blk).wait_send()


def on_device(far, near, n_pts, points, centroids):
    steps, own, dim = points.shape
    k_loc = centroids.shape[0]
    n_blk = k_loc // ROWS
    batch = far * near * own
    groups = batch // LANES
    vmem = pl.BlockSpec(memory_space=pltpu.VMEM)
    dma = pltpu.SemaphoreType.DMA
    return pl.pallas_call(
        functools.partial(kernel, far, near, n_pts),
        out_shape=(pltpu.VMEM((k_loc, dim), jnp.float32),
                   pltpu.VMEM((steps, batch), jnp.float32)),
        in_specs=[pl.BlockSpec(memory_space=pl.ANY)] * 2,
        out_specs=(vmem, vmem),
        scratch_shapes=[
            pltpu.VMEM((steps, far, near * own, dim), jnp.bfloat16),
            pltpu.VMEM((k_loc, batch), jnp.float32),
            pltpu.VMEM((k_loc, dim), jnp.float32),
            pltpu.VMEM((k_loc, dim), jnp.bfloat16),
            pltpu.VMEM((k_loc, LANES), jnp.float32),
            pltpu.VMEM((steps, far * near, 2, groups, LANES), jnp.float32),
            pltpu.VMEM((steps, n_pts, n_blk, ROWS + 8, dim), jnp.float32),
            dma((steps, far)),
            dma((steps, far, near)),
            dma((steps, far, near)),
            dma((steps, far * near)),
            dma((steps, far * near)),
            dma((steps, n_pts, n_blk)),
            dma((steps, n_pts, n_blk)),
            dma((steps,)),
            dma((n_blk,)),
        ],
        compiler_params=pltpu.CompilerParams(
            collective_id=0, has_side_effects=True, vmem_limit_bytes=60 * 1024 * 1024),
    )(points, centroids)


def solution(mesh):
    far, near = split(mesh.shape["cen"])
    placed = (P(None, ("pts", "cen"), None), P("cen", None))
    return jax.shard_map(
        functools.partial(on_device, far, near, mesh.shape["pts"]),
        mesh=mesh,
        in_specs=placed,
        out_specs=(P("cen", None), P(None, "pts")),
        check_vma=False,
    )
```

```python
import functools

import jax
import jax.numpy as jnp
from jax import lax
from jax.experimental import pallas as pl
from jax.experimental.pallas import tpu as pltpu
from jax.sharding import PartitionSpec as P

TEMPER = 32.0
MESH = pl.DeviceIdType.MESH
LANES = 128
ROWS = 256


def split(n):
    near = 1
    while near * near * 4 <= n:
        near *= 2
    assert n % near == 0 and (n // near) & (n // near - 1) == 0
    return n // near, near


def flip(i, d):
    bit = 1
    while bit <= d:
        if d & bit:
            i = i + bit - 2 * bit * lax.rem(i // bit, 2)
        bit *= 2
    return i


def kernel(far, near, n_pts, pts_ref, cen_ref, out_ref, en_ref,
           x_ref, w_ref, cur_ref, low_ref, sq_ref, stat, got,
           z_send, q_send, p_recv, s_send, s_recv, c_send, c_recv,
           in_sem, cen_sem):
    steps, own, dim = pts_ref.shape
    k_loc = cen_ref.shape[0]
    n_blk = k_loc // ROWS
    width = near * own
    cols = width // LANES
    groups = far * cols
    cen = lax.axis_index("cen")
    p = lax.axis_index("pts")
    a = cen // near
    b = lax.rem(cen, near)
    far_peers = [flip(a, d) for d in range(1, far)]
    near_peers = [flip(b, d) for d in range(1, near)]
    pts_peers = [lax.rem(p + d, n_pts) for d in range(1, n_pts)]

    barrier = pltpu.get_barrier_semaphore()
    for peer in far_peers:
        pl.semaphore_signal(barrier, inc=1, device_id={"cen": peer * near + b}, device_id_type=MESH)
    for peer in near_peers:
        pl.semaphore_signal(barrier, inc=1, device_id={"cen": a * near + peer}, device_id_type=MESH)
    for peer in pts_peers:
        pl.semaphore_signal(barrier, inc=1, device_id={"pts": peer}, device_id_type=MESH)

    def lowered(value):
        low = value.astype(jnp.bfloat16).astype(jnp.float32) * (2.0 / TEMPER)
        sq = jnp.sum(value * value, axis=1, keepdims=True) * (1.0 / TEMPER)
        return low.astype(jnp.bfloat16), sq

    def cen_copy(blk):
        rows = pl.ds(pl.multiple_of(blk * ROWS, ROWS), ROWS)
        return pltpu.make_async_copy(cen_ref.at[rows, :], cur_ref.at[rows, :], cen_sem.at[blk])

    def pts_copy(s):
        return pltpu.make_async_copy(pts_ref.at[s], x_ref.at[s, a, pl.ds(b * own, own), :], in_sem.at[s])

    for s in range(steps):
        pts_copy(s).start()

    @pl.loop(0, n_blk)
    def _(blk):
        cen_copy(blk).start()

    for s in range(steps):
        pts_copy(s).wait()

    @pl.loop(0, n_blk)
    def _(blk):
        cen_copy(blk).wait()
        rows = pl.ds(pl.multiple_of(blk * ROWS, ROWS), ROWS)
        low_ref[rows, :], sq = lowered(cur_ref[rows, :])
        sq_ref[rows, :] = jnp.broadcast_to(sq, (ROWS, LANES))

    pl.semaphore_wait(barrier, len(far_peers) + len(near_peers) + len(pts_peers))

    def chunk(s, i, j):
        return x_ref.at[s, i, pl.ds(j * own, own), :]

    def far_copy(s, d):
        peer = flip(a, d)
        return pltpu.make_async_remote_copy(
            src_ref=chunk(s, a, b), dst_ref=chunk(s, a, b),
            send_sem=z_send.at[s, d], recv_sem=p_recv.at[s, a, b],
            device_id={"cen": peer * near + b}, device_id_type=MESH)

    def near_copy(s, i, d):
        peer = flip(b, d)
        return pltpu.make_async_remote_copy(
            src_ref=chunk(s, i, b), dst_ref=chunk(s, i, b),
            send_sem=q_send.at[s, i, d], recv_sem=p_recv.at[s, i, b],
            device_id={"cen": a * near + peer}, device_id_type=MESH)

    def own_near_copy(s, d):
        peer = flip(b, d)
        return pltpu.make_async_remote_copy(
            src_ref=chunk(s, a, b), dst_ref=chunk(s, a, b),
            send_sem=q_send.at[s, a, d], recv_sem=p_recv.at[s, a, b],
            device_id={"cen": a * near + peer}, device_id_type=MESH)

    def arrived(s, i, j):
        pltpu.make_async_remote_copy(
            src_ref=chunk(s, i, j), dst_ref=chunk(s, i, j),
            send_sem=z_send.at[s, 0], recv_sem=p_recv.at[s, i, j],
            device_id={"cen": cen}, device_id_type=MESH).wait_recv()

    def send_own(s):
        for d in reversed(range(1, far)):
            far_copy(s, d).start()
        for d in reversed(range(1, near)):
            own_near_copy(s, d).start()

    def forward(s):
        for d in range(1, far):
            i = flip(a, d)
            arrived(s, i, b)
            for e in reversed(range(1, near)):
                near_copy(s, i, e).start()

    def stat_copy(s, d):
        return pltpu.make_async_remote_copy(
            src_ref=stat.at[s, cen], dst_ref=stat.at[s, cen],
            send_sem=s_send.at[s, d], recv_sem=s_recv.at[s, cen],
            device_id={"cen": flip(cen, d)}, device_id_type=MESH)

    def sums_copy(s, d, blk):
        peer = lax.rem(p + d, n_pts)
        return pltpu.make_async_remote_copy(
            src_ref=got.at[s, p, blk], dst_ref=got.at[s, p, blk],
            send_sem=c_send.at[s, d, blk], recv_sem=c_recv.at[s, p, blk],
            device_id={"pts": peer}, device_id_type=MESH)

    def landed(ref, sem):
        pltpu.make_async_remote_copy(
            src_ref=ref, dst_ref=ref, send_sem=z_send.at[0, 0], recv_sem=sem,
            device_id={"cen": cen}, device_id_type=MESH).wait_recv()

    def joined(s):
        tops = stat[s, :, 0]
        top = jnp.max(tops, axis=0)
        return top, jnp.sum(stat[s, :, 1] * jnp.exp(tops - top[None]), axis=0)

    send_own(0)
    forward(0)
    send_own(1) if steps > 1 else None

    for s in range(steps):
        def one_group(i):
            for e in range(1, near):
                arrived(s, i, flip(b, e))
            for j in range(cols):
                xg = x_ref[s, i, j * LANES:(j + 1) * LANES, :]
                logits = lax.dot_general(
                    low_ref[...], xg, (((1,), (1,)), ((), ())),
                    preferred_element_type=jnp.float32) - sq_ref[...]
                top = jnp.max(logits, axis=0, keepdims=True)
                weights = jnp.exp(logits - top)
                g = i * cols + j
                w_ref[:, pl.ds(pl.multiple_of(g * LANES, LANES), LANES)] = weights
                stat[s, cen, 0, pl.ds(g, 1), :] = top
                stat[s, cen, 1, pl.ds(g, 1), :] = jnp.sum(weights, axis=0, keepdims=True)

        if s == 0:
            for d in range(far):
                one_group(flip(a, d))
        for d in reversed(range(1, far * near)):
            stat_copy(s, d).start()
        if s + 1 < steps:
            forward(s + 1)
            if s + 2 < steps:
                send_own(s + 2)
        for d in range(1, far * near):
            i = flip(cen, d)
            landed(stat.at[s, i], s_recv.at[s, i])
        top, total = joined(s)
        energy = top + jnp.log(total)
        scale = jnp.exp(stat[s, cen, 0] - top) / total
        for g in range(groups):
            en_ref[s:s + 1, g * LANES:(g + 1) * LANES] = energy[g:g + 1, :]
        scale = jnp.concatenate([scale[g:g + 1, :] for g in range(groups)], axis=1)

        @pl.loop(0, n_blk)
        def _(blk):
            rows = pl.ds(pl.multiple_of(blk * ROWS, ROWS), ROWS)
            resp = w_ref[rows, :] * scale
            part = resp[:, :LANES]
            for g in range(1, groups):
                part = part + resp[:, g * LANES:(g + 1) * LANES]
            count = jnp.sum(jnp.transpose(part), axis=0, keepdims=True)
            xs = x_ref[s].reshape(far * width, dim)
            sums = lax.dot_general(
                resp.astype(jnp.bfloat16), xs, (((1,), (0,)), ((), ())),
                preferred_element_type=jnp.float32)
            got[s, p, blk, :ROWS, :] = sums
            got[s, p, blk, ROWS:ROWS + 1, :] = count
            for d in range(1, n_pts):
                sums_copy(s, d, blk).start()

        if s + 1 < steps:
            for d in range(far):
                for e in range(1, near):
                    arrived(s + 1, flip(a, d), flip(b, e))

        def finish(blk, top):
            rows = pl.ds(pl.multiple_of(blk * ROWS, ROWS), ROWS)
            for d in range(1, n_pts):
                i = lax.rem(p + d, n_pts)
                landed(got.at[s, i, blk], c_recv.at[s, i, blk])
            sums = got[s, 0, blk, :ROWS, :]
            count = got[s, 0, blk, ROWS:ROWS + 1, :]
            for i in range(1, n_pts):
                sums = sums + got[s, i, blk, :ROWS, :]
                count = count + got[s, i, blk, ROWS:ROWS + 1, :]
            column = jnp.transpose(jnp.broadcast_to(1.0 + count, (LANES, ROWS)))
            column = jnp.concatenate([column] * (dim // LANES), axis=1)
            value = (cur_ref[rows, :] + sums) / column
            if s + 1 == steps:
                out_ref[rows, :] = value
                return top
            cur_ref[rows, :] = value
            low, sq = lowered(value)
            logits = lax.dot_general(
                low, x_ref[s + 1].reshape(far * width, dim), (((1,), (1,)), ((), ())),
                preferred_element_type=jnp.float32) - sq
            w_ref[rows, :] = logits
            return jnp.maximum(top, jnp.max(logits, axis=0, keepdims=True))

        def weigh(top, blk, total):
            rows = pl.ds(pl.multiple_of(blk * ROWS, ROWS), ROWS)
            weights = jnp.exp(w_ref[rows, :] - top)
            w_ref[rows, :] = weights
            return total + jnp.sum(weights, axis=0, keepdims=True)

        top = lax.fori_loop(0, n_blk, finish, jnp.full((1, groups * LANES), -jnp.inf, jnp.float32))
        if s + 1 < steps:
            total = lax.fori_loop(0, n_blk, functools.partial(weigh, top), jnp.zeros_like(top))
            for g in range(groups):
                stat[s + 1, cen, 0, g:g + 1, :] = top[:, g * LANES:(g + 1) * LANES]
                stat[s + 1, cen, 1, g:g + 1, :] = total[:, g * LANES:(g + 1) * LANES]

    for s in range(steps):
        for d in range(1, far * near):
            stat_copy(s, d).wait_send()
        for d in range(1, far):
            far_copy(s, d).wait_send()
            for e in range(1, near):
                near_copy(s, flip(a, d), e).wait_send()
        for d in range(1, near):
            own_near_copy(s, d).wait_send()

        @pl.loop(0, n_blk)
        def _(blk):
            for d in range(1, n_pts):
                sums_copy(s, d, blk).wait_send()


def on_device(far, near, n_pts, points, centroids):
    steps, own, dim = points.shape
    k_loc = centroids.shape[0]
    n_blk = k_loc // ROWS
    batch = far * near * own
    groups = batch // LANES
    vmem = pl.BlockSpec(memory_space=pltpu.VMEM)
    dma = pltpu.SemaphoreType.DMA
    return pl.pallas_call(
        functools.partial(kernel, far, near, n_pts),
        out_shape=(pltpu.VMEM((k_loc, dim), jnp.float32),
                   pltpu.VMEM((steps, batch), jnp.float32)),
        in_specs=[pl.BlockSpec(memory_space=pl.ANY)] * 2,
        out_specs=(vmem, vmem),
        scratch_shapes=[
            pltpu.VMEM((steps, far, near * own, dim), jnp.bfloat16),
            pltpu.VMEM((k_loc, batch), jnp.float32),
            pltpu.VMEM((k_loc, dim), jnp.float32),
            pltpu.VMEM((k_loc, dim), jnp.bfloat16),
            pltpu.VMEM((k_loc, LANES), jnp.float32),
            pltpu.VMEM((steps, far * near, 2, groups, LANES), jnp.float32),
            pltpu.VMEM((steps, n_pts, n_blk, ROWS + 8, dim), jnp.float32),
            dma((steps, far)),
            dma((steps, far, near)),
            dma((steps, far, near)),
            dma((steps, far * near)),
            dma((steps, far * near)),
            dma((steps, n_pts, n_blk)),
            dma((steps, n_pts, n_blk)),
            dma((steps,)),
            dma((n_blk,)),
        ],
        compiler_params=pltpu.CompilerParams(
            collective_id=0, has_side_effects=True, vmem_limit_bytes=60 * 1024 * 1024),
    )(points, centroids)


def solution(mesh):
    far, near = split(mesh.shape["cen"])
    placed = (P(None, ("pts", "cen"), None), P("cen", None))
    return jax.shard_map(
        functools.partial(on_device, far, near, mesh.shape["pts"]),
        mesh=mesh,
        in_specs=placed,
        out_specs=(P("cen", None), P(None, "pts")),
        check_vma=False,
    )
```
